1024 devices in a mesh: row: 32 (over x, y), col: 32 (over z, core).
Axes of the slice: x: 4, y: 8, z: 16, core: 2. Of those that a mesh axis runs over, the one named last changes fastest.
Arguments:
- x_block: bfloat16 [64, 262144], P(None, ('col', 'row')), may hold values from -6 to 6
- tiles: bfloat16 [24576, 256, 256], P(('row', 'col')), may hold values from -0.078125 to 0.078125
- coords: int32 [24576, 2], P(('row', 'col')), may hold values from 0 to 31, as said below
- counts: int32 [1024], P(('row', 'col')), may hold values from 9 to 24, as said below
Outputs:
- basis: float32 [64, 262144], P(None, ('row', 'col'))
- factor: float32 [64, 64], replicated
The draws below stay inside these ranges and needn't reach their ends.
Inputs may be any that keep to these rules, and one draw needn't show every extreme that they name: `coords`: column 0 is a tile row below 32, column 1 a tile column below 32; at the device of place p = i * 32 + j, slot 0 names tile row j. `counts`: some device uses all 24 slots.
All inputs are finite; a program needn't handle non-finite values.
Results may differ from the reference program's by a relative error of at most 0.0003.
Values may be sent and summed in bfloat16 or wider, within the bound.
A program may use at most 32 MiB of HBM per device.

```python
import jax
import jax.numpy as jnp
from jax import lax

COLS = 64
TILE = 256
KMAX = 24
N = 262144
PIECES = 1024
PIECE_TILES = 1
ROW_TILES = 32
COL_TILES = 32
SLOTS = 24576
N_COL = 32


def draw_coords(key, part):
    first_key, second_key = jax.random.split(key)
    tile_rows = jax.random.randint(first_key, (PIECES, KMAX), 0, ROW_TILES, dtype=jnp.int32)
    tile_cols = jax.random.randint(second_key, (PIECES, KMAX), 0, COL_TILES, dtype=jnp.int32)
    device = jnp.arange(PIECES, dtype=jnp.int32)[:, None]
    slot_index = jnp.arange(KMAX, dtype=jnp.int32)[None, :]
    column_place = device % (ROW_TILES // PIECE_TILES)
    own_rows = column_place * PIECE_TILES + slot_index
    tile_rows = jnp.where(slot_index < PIECE_TILES, own_rows, tile_rows)
    return jnp.stack([tile_rows, tile_cols], axis=-1).reshape(PIECES * KMAX, 2)


def draw_counts(key, part):
    first_key, second_key = jax.random.split(key)
    lowest = max(PIECE_TILES, 2 * KMAX // 5)
    values = jax.random.randint(first_key, (PIECES,), lowest, KMAX + 1, dtype=jnp.int32)
    busiest = jax.random.randint(second_key, (), 0, PIECES, dtype=jnp.int32)
    return values.at[busiest].set(KMAX)


def levels(stream_key, extent, cuts, least, high):
    def one(dim, blocks):
        draws = jax.random.uniform(jax.random.fold_in(jax.random.fold_in(stream_key, 6), dim), (blocks,), jnp.float32, least / len(cuts), high / len(cuts))
        return jnp.repeat(jnp.exp(draws), extent[dim] // blocks).reshape((-1,) + (1,) * (len(extent) - dim - 1))

    factor_of = one(*cuts[0])
    for cut in cuts[1:]:
        factor_of = factor_of * one(*cut)
    return factor_of


def gaussian(key, dims, spread, most, pieces=(), held_as=jnp.bfloat16):
    values = jax.random.normal(key, dims, jnp.float32) * spread
    if len(pieces) > 0:
        values = levels(key, dims, pieces, -0.22, 0.18) * values
    return jnp.clip(values, min=-most, max=most).astype(held_as)


def setup_inputs(seed: int = 0) -> dict:
    seeds = jax.random.split(jax.random.key(seed), 5)
    return {
        "x_block": gaussian(seeds[0], (COLS, N), 1.0, 6.0, ((1, 1024),)),
        "tiles": gaussian(seeds[1], (SLOTS, TILE, TILE), (TILE * KMAX) ** -0.5, 0.078125, ((0, 1024),)),
        "coords": draw_coords(jax.random.fold_in(seeds[4], 71), 0),
        "counts": draw_counts(jax.random.fold_in(seeds[4], 71), 0),
    }


def block_product(block_cols, slot_tiles, slot_coords, slot_count):
    vector_count = block_cols.shape[0]
    tile_size = slot_tiles.shape[1]
    shaped = block_cols.reshape(vector_count, COL_TILES, tile_size)
    picked = jnp.take(shaped, slot_coords[:, 1], axis=1).astype(jnp.float32)
    contrib = jnp.einsum('ckj,kij->kci', picked, slot_tiles.astype(jnp.float32), precision=lax.Precision.HIGHEST)
    live_slots = jnp.arange(KMAX, dtype=jnp.int32) < slot_count
    onehot = ((slot_coords[:, 0][None, :] == jnp.arange(ROW_TILES, dtype=jnp.int32)[:, None]) & live_slots[None, :]).astype(jnp.float32)
    summed = jnp.einsum('rk,kci->cri', onehot, contrib, precision=lax.Precision.HIGHEST)
    return summed.reshape(vector_count, ROW_TILES * tile_size)

def reference(x_block, tiles, coords, counts):
    vector_count = x_block.shape[0]
    block_rows = ROW_TILES * TILE
    block_width = COL_TILES * TILE
    tiles_all = tiles.reshape(PIECES, KMAX, TILE, TILE)
    coords_all = coords.reshape(PIECES, KMAX, 2)

    def accumulate(running, inputs):
        device, slot_tiles, slot_coords, slot_count = inputs
        block_row = device // N_COL
        block_col = device % N_COL
        block_cols = lax.dynamic_slice_in_dim(x_block, (block_col * block_width).astype(jnp.int32), block_width, 1)
        partial_rows = block_product(block_cols, slot_tiles, slot_coords, slot_count)
        start = (block_row * block_rows).astype(jnp.int32)
        before = lax.dynamic_slice_in_dim(running, start, block_rows, 1)
        running = lax.dynamic_update_slice_in_dim(running, before + partial_rows, start, 1)
        return (running, None)
    initial = jnp.zeros((vector_count, N), jnp.float32)
    devices_index = jnp.arange(PIECES, dtype=jnp.int32)
    y_full, _ = lax.scan(accumulate, initial, (devices_index, tiles_all, coords_all, counts))
    gram_total = jnp.dot(y_full.astype(jnp.float32), y_full.T.astype(jnp.float32), precision=lax.Precision.HIGHEST, preferred_element_type=jnp.float32) / N
    lower_factor = jnp.linalg.cholesky(gram_total)
    basis = jax.scipy.linalg.solve_triangular(lower_factor, y_full, lower=True)
    return (basis, lower_factor.T)
```

```python
import functools

import jax
import jax.numpy as jnp
from jax import lax
from jax.experimental import pallas as pl
from jax.experimental.pallas import tpu as pltpu
from jax.sharding import PartitionSpec as P

MESH = pl.DeviceIdType.MESH
HIGH = lax.Precision.HIGHEST
NT = (((1,), (1,)), ((), ()))
DIMS = (4, 8, 16)


def far_first(n):
    return sorted(range(1, n), key=lambda k: -min(k, n - k))


def exchange(
    dims, slots, total, table, x_hbm, tiles_hbm, gram_ref, y_ref,
    blocks, tiles, acc, give, take, ring_out, ring_in, pack, gin, yin, zin, gall, cut,
    local_sem, ay_s, ay_r, ax_s, ax_r, ex_s, ex_r, ring_s, ring_r, g_s, g_r, gy_s, gy_r, gz_s, gz_r, f_s, f_r,
):
    nx, ny, nz = dims
    half = nz // 2
    row, col = lax.axis_index("row"), lax.axis_index("col")
    x, y = row // ny, row % ny
    z, c = col // 2, col % 2
    vecs = y_ref.shape[0]
    part = vecs // 2

    def at(dx=0, dy=0, dz=0, dc=0):
        return (lax.rem(x + dx, nx) * ny + lax.rem(y + dy, ny), lax.rem(z + dz, nz) * 2 + lax.rem(c + dc, 2))

    def copy(src, dst, send, recv, dev):
        return pltpu.make_async_remote_copy(
            src_ref=src, dst_ref=dst, send_sem=send, recv_sem=recv, device_id=dev, device_id_type=MESH
        )

    near = [at(dy=k) for k in range(1, ny)] + [at(dx=k) for k in range(1, nx)]
    near += [at(dc=1), at(dz=1), at(dz=nz - 1)]
    barrier = pltpu.get_barrier_semaphore()
    for dev in near:
        pl.semaphore_signal(barrier, inc=1, device_id=dev, device_id_type=MESH)
    get_x = pltpu.make_async_copy(x_hbm, blocks.at[row], local_sem.at[0])
    get_x.start()
    get_tiles = pltpu.make_async_copy(tiles_hbm, tiles, local_sem.at[1])
    get_tiles.start()
    acc[slots] = jnp.zeros_like(acc[slots])
    get_x.wait()
    pl.semaphore_wait(barrier, len(near))

    def gather_y(k):
        return copy(blocks.at[row], blocks.at[row], ay_s.at[k], ay_r.at[k], at(dy=k))

    def landed_y(k):
        slot = blocks.at[x * ny + lax.rem(y + ny - k, ny)]
        return copy(slot, slot, ay_s.at[k], ay_r.at[k], at(dy=k))

    def gather_x(k, m):
        slot = blocks.at[x * ny + lax.rem(y + ny - k, ny)]
        return copy(slot, slot, ax_s.at[k, m], ax_r.at[k, m], at(dx=m))

    def landed_x(k, m):
        slot = blocks.at[lax.rem(x + nx - m, nx) * ny + lax.rem(y + ny - k, ny)]
        return copy(slot, slot, ax_s.at[k, m], ax_r.at[k, m], at(dx=m))

    for k in far_first(ny):
        gather_y(k).start()
    for m in far_first(nx):
        gather_x(0, m).start()
    for k in reversed(far_first(ny)):
        landed_y(k).wait_recv()
        for m in far_first(nx):
            gather_x(k, m).start()
    for k in [0] + list(reversed(far_first(ny))):
        for m in range(1, nx):
            landed_x(k, m).wait_recv()
    get_tiles.wait()

    def product(g, carry):
        for u in range(4):
            k = g * 4 + u
            acc[k] = lax.dot_general(
                blocks[table[k]], tiles[k], NT, preferred_element_type=jnp.float32
            )
        return carry

    lax.fori_loop(0, slots // 4, product, 0)

    def chain(k, carry):
        acc[k] = acc[k] + acc[table[slots + k]]
        return carry

    lax.fori_loop(0, slots, chain, 0)

    def partial(d, core):
        return acc[table[2 * slots + lax.rem(z + d, nz) * 2 + core]]

    def swap(d):
        return copy(give.at[d], take.at[d], ex_s.at[d], ex_r.at[d], at(dc=1))

    def offset(n):
        return lax.rem(nz + half + jnp.where(n % 2 == 0, n // 2, nz - (n + 1) // 2), nz)

    def hand(n, carry):
        d = offset(n)
        give[d] = partial(d, 1 - c)
        swap(d).start()
        return carry

    lax.fori_loop(0, nz, hand, 0)

    def own(d):
        swap(d).wait_recv()
        return partial(d, c) + take[d]

    top, low = pl.ds(0, part), pl.ds(part, part)

    def hop(way, s, h):
        rows = pl.ds(h * part, part)
        return copy(
            ring_out.at[way, s, rows], ring_in.at[way, s, rows], ring_s.at[way, s, h], ring_r.at[way, s, h],
            at(dz=1 if way == 0 else nz - 1),
        )

    v = own(half)
    ring_out[0, 0, top] = v[:part]
    hop(0, 0, 0).start()
    ring_out[1, 0, low] = v[part:]
    hop(1, 0, 1).start()

    def fill(s, carry):
        ring_out[0, s] = own(half - s)
        ring_out[1, s] = own(half + s)
        return carry

    lax.fori_loop(1, half, fill, 0)
    y_ref[...] = own(0)
    hop(0, 1, 1).start()
    hop(1, 1, 0).start()
    hop(0, 0, 0).wait_recv()
    ring_out[0, 1, top] += ring_in[0, 0, top]
    hop(0, 1, 0).start()
    hop(1, 0, 1).wait_recv()
    ring_out[1, 1, low] += ring_in[1, 0, low]
    hop(1, 1, 1).start()

    def step(s, carry):
        for h in range(2):
            for way in range(2):
                rows = top if (h == 0) == (way == 1) else low
                g = h if way == 1 else 1 - h
                hop(way, s - 1, g).wait_recv()
                ring_out[way, s, rows] += ring_in[way, s - 1, rows]
                hop(way, s, g).start()
        return carry

    lax.fori_loop(2, half, step, 0)
    for way in range(2):
        for h in range(2):
            hop(way, half - 1, h).wait_recv()
    whole = y_ref[...] + ring_in[0, half - 1] + ring_in[1, half - 1]
    y_ref[...] = whole

    gram = lax.dot_general(whole, whole, NT, precision=HIGH, preferred_element_type=jnp.float32) * (1.0 / total)
    wide = jnp.concatenate([gram[:part], gram[part:]], axis=1)
    parts = nx * 2
    rows = part // parts
    mine = x * 2 + c
    for q in range(parts):
        pack[q] = wide[q * rows : (q + 1) * rows]

    around = [(dx, dc) for dx in range(nx) for dc in range(2) if (dx, dc) != (0, 0)]

    def place(dx, dc):
        return lax.rem(x + dx, nx) * 2 + lax.rem(c + dc, 2)

    def spread(dx, dc):
        n = dx * 2 + dc
        return copy(pack.at[place(dx, dc)], gin.at[mine], g_s.at[n], g_r.at[n], at(dx=dx, dc=dc))

    for dx, dc in around:
        spread(dx, dc).start()
    gin[mine] = pack[mine]
    for dx, dc in around:
        spread(dx, dc).wait_recv()
    s = gin[0]
    for q in range(1, parts):
        s = s + gin[q]
    yin[y] = s

    def over_y(k):
        return copy(yin.at[y], yin.at[y], gy_s.at[k], gy_r.at[k], at(dy=k))

    for k in far_first(ny):
        over_y(k).start()
    for k in range(1, ny):
        slot = yin.at[lax.rem(y + ny - k, ny)]
        copy(slot, slot, gy_s.at[k], gy_r.at[k], at(dy=k)).wait_recv()
    s = yin[0]
    for q in range(1, ny):
        s = s + yin[q]
    zin[z] = s

    def over_z(k):
        return copy(zin.at[z], zin.at[z], gz_s.at[k], gz_r.at[k], at(dz=k))

    for k in far_first(nz):
        over_z(k).start()
    for k in range(1, nz):
        slot = zin.at[lax.rem(z + nz - k, nz)]
        copy(slot, slot, gz_s.at[k], gz_r.at[k], at(dz=k)).wait_recv()
    s = zin[0]
    for q in range(1, nz):
        s = s + zin[q]
    gall[mine] = s

    def collect(dx, dc):
        n = dx * 2 + dc
        return copy(gall.at[mine], gall.at[mine], f_s.at[n], f_r.at[n], at(dx=dx, dc=dc))

    for dx, dc in around:
        collect(dx, dc).start()
    for dx, dc in around:
        n = dx * 2 + dc
        slot = gall.at[lax.rem(x + nx - dx, nx) * 2 + lax.rem(c + dc, 2)]
        copy(slot, slot, f_s.at[n], f_r.at[n], at(dx=dx, dc=dc)).wait_recv()
    for q in range(parts):
        gram_ref[q * rows : (q + 1) * rows] = gall[q]

    for k in range(1, ny):
        gather_y(k).wait_send()
        over_y(k).wait_send()
    for k in range(ny):
        for m in range(1, nx):
            gather_x(k, m).wait_send()
    for k in range(1, nz):
        over_z(k).wait_send()
    for dx, dc in around:
        spread(dx, dc).wait_send()
        collect(dx, dc).wait_send()

    def drain(d, carry):
        swap(d).wait_send()
        return carry

    lax.fori_loop(0, nz, drain, 0)
    hop(0, 0, 0).wait_send()
    hop(1, 0, 1).wait_send()

    def drain_ring(s, carry):
        for way in range(2):
            for h in range(2):
                hop(way, s, h).wait_send()
        return carry

    lax.fori_loop(1, half, drain_ring, 0)


def orthonormal(gram_ref, y_ref, basis_ref, factor_ref):
    n = y_ref.shape[0]
    half = n // 2
    packed = gram_ref[...]
    gram = jnp.concatenate([packed[:, :n], packed[:, n:]], axis=0)
    lane = lax.broadcasted_iota(jnp.int32, (n, n), 1)
    line = lax.broadcasted_iota(jnp.int32, (n, n), 0)
    work = jnp.concatenate([gram, (lane == line).astype(jnp.float32)], axis=1)
    groups = [work[g * 8 : (g + 1) * 8] for g in range(n // 8)]
    sub = lax.broadcasted_iota(jnp.int32, (8, 1), 0)
    for k in range(n):
        g, r = k // 8, k % 8
        pivot_row = groups[g][r : r + 1]
        scaled = pivot_row / pivot_row[:, k : k + 1]
        for i in range(g, n // 8):
            column = groups[i][:, k : k + 1]
            if i == g:
                column = jnp.where(sub > r, column, 0.0)
            groups[i] = groups[i] - column * scaled
    done = jnp.concatenate(groups, axis=0)
    diag = jnp.sum(jnp.where(lane == line, done[:, :n], 0.0), axis=1, keepdims=True)
    done = done / jnp.sqrt(diag)
    factor_ref[...] = jnp.where(lane >= line, done[:, :n], 0.0)
    basis_ref[...] = jnp.dot(done[:, n:], y_ref[...], precision=HIGH, preferred_element_type=jnp.float32)


def local(dims, x_block, tiles, coords, counts):
    nx, ny, nz = dims
    vecs, width = x_block.shape
    slots = tiles.shape[0]
    lines = 2 * nz
    half = nz // 2
    parts = nx * 2
    rows = vecs // 2 // parts
    total = width * nx * ny * nz * 2
    order = jnp.arange(slots, dtype=jnp.int32)
    live = order < counts[0]
    wanted = jnp.concatenate([coords[:, 0], jnp.arange(lines, dtype=jnp.int32)])
    limit = jnp.concatenate([order, jnp.full((lines,), slots, jnp.int32)])
    hit = (wanted[:, None] == coords[:, 0][None, :]) & live[None, :] & (order[None, :] < limit[:, None])
    last = jnp.max(jnp.where(hit, order[None, :], -1), axis=1)
    table = jnp.concatenate([coords[:, 1], jnp.where(last < 0, slots, last)])
    dma = pltpu.SemaphoreType.DMA
    f32 = jnp.float32
    gram, y = pl.pallas_call(
        functools.partial(exchange, dims, slots, total),
        name="exchange",
        out_shape=(jax.ShapeDtypeStruct((vecs // 2, 2 * vecs), f32), jax.ShapeDtypeStruct((vecs, width), f32)),
        in_specs=[
            pl.BlockSpec(memory_space=pltpu.SMEM),
            pl.BlockSpec(memory_space=pl.ANY),
            pl.BlockSpec(memory_space=pl.ANY),
        ],
        out_specs=(pl.BlockSpec(memory_space=pltpu.VMEM), pl.BlockSpec(memory_space=pltpu.VMEM)),
        scratch_shapes=[
            pltpu.VMEM((nx * ny, vecs, width), jnp.bfloat16),
            pltpu.VMEM(tiles.shape, jnp.bfloat16),
            pltpu.VMEM((slots + 1, vecs, width), f32),
            pltpu.VMEM((nz, vecs, width), f32),
            pltpu.VMEM((nz, vecs, width), f32),
            pltpu.VMEM((2, half, vecs, width), f32),
            pltpu.VMEM((2, half, vecs, width), f32),
            pltpu.VMEM((parts, rows, 2 * vecs), f32),
            pltpu.VMEM((parts, rows, 2 * vecs), f32),
            pltpu.VMEM((ny, rows, 2 * vecs), f32),
            pltpu.VMEM((nz, rows, 2 * vecs), f32),
            pltpu.VMEM((parts, rows, 2 * vecs), f32),
            pltpu.VMEM((8, 128), f32),
            dma((2,)),
            dma((ny,)), dma((ny,)),
            dma((ny, nx)), dma((ny, nx)),
            dma((nz,)), dma((nz,)),
            dma((2, half, 2)), dma((2, half, 2)),
            dma((parts,)), dma((parts,)),
            dma((ny,)), dma((ny,)),
            dma((nz,)), dma((nz,)),
            dma((parts,)), dma((parts,)),
        ],
        compiler_params=pltpu.CompilerParams(
            collective_id=0, has_side_effects=True, vmem_limit_bytes=48 * 1024 * 1024
        ),
    )(table, x_block, tiles)
    return pl.pallas_call(
        orthonormal,
        name="orthonormal",
        out_shape=(jax.ShapeDtypeStruct((vecs, width), f32), jax.ShapeDtypeStruct((vecs, vecs), f32)),
        in_specs=[pl.BlockSpec(memory_space=pltpu.VMEM)] * 2,
        out_specs=(pl.BlockSpec(memory_space=pltpu.VMEM), pl.BlockSpec(memory_space=pltpu.VMEM)),
    )(gram, y)


def solution(mesh):
    placed = (
        P(None, ("col", "row")),
        P(("row", "col"), None, None),
        P(("row", "col"), None),
        P(("row", "col")),
    )
    return jax.shard_map(
        functools.partial(local, DIMS),
        mesh=mesh,
        in_specs=placed,
        out_specs=(P(None, ("row", "col")), P()),
        check_vma=False,
    )
```

```python
import functools

import jax
import jax.numpy as jnp
from jax import lax
from jax.experimental import pallas as pl
from jax.experimental.pallas import tpu as pltpu
from jax.sharding import PartitionSpec as P

MESH = pl.DeviceIdType.MESH
HIGH = lax.Precision.HIGHEST
NT = (((1,), (1,)), ((), ()))
DIMS = (4, 8, 16)


NEAR = 3
CHUNKS = 4


def near_first(n):
    return sorted(range(1, n), key=lambda k: min(k, n - k))


def far_first(n):
    return near_first(n)[::-1]


def exchange(
    dims, slots, total, coords, counts, x_hbm, tiles_hbm, gram_ref, y_ref,
    table, blocks, tiles, acc, give, take, ring_out, ring_in, pack, gin, yin, zin, gall,
    local_sem, ay_s, ay_r, ax_s, ax_r, ex_s, ex_r, ring_s, ring_r, g_s, g_r, gy_s, gy_r, gz_s, gz_r, f_s, f_r,
):
    nx, ny, nz = dims
    half = nz // 2
    row, col = lax.axis_index("row"), lax.axis_index("col")
    x, y = row // ny, row % ny
    z, c = col // 2, col % 2
    vecs = y_ref.shape[0]
    part = vecs // 2

    def at(dx=0, dy=0, dz=0, dc=0):
        return (lax.rem(x + dx, nx) * ny + lax.rem(y + dy, ny), lax.rem(z + dz, nz) * 2 + lax.rem(c + dc, 2))

    def copy(src, dst, send, recv, dev):
        return pltpu.make_async_remote_copy(
            src_ref=src, dst_ref=dst, send_sem=send, recv_sem=recv, device_id=dev, device_id_type=MESH
        )

    near = max(0, min(NEAR, half - 2))
    peers = [at(dy=k) for k in range(1, ny)] + [at(dx=k) for k in range(1, nx)] + [at(dc=1)]
    peers += [at(dz=k) for k in sorted({1, near + 1, nz - near - 1, nz - 1})]
    barrier = pltpu.get_barrier_semaphore()
    for dev in peers:
        pl.semaphore_signal(barrier, inc=1, device_id=dev, device_id_type=MESH)
    get_x = pltpu.make_async_copy(x_hbm, blocks.at[row], local_sem.at[0])
    get_x.start()
    get_tiles = pltpu.make_async_copy(tiles_hbm, tiles, local_sem.at[1])
    get_tiles.start()
    acc[slots] = jnp.zeros_like(acc[slots])
    get_x.wait()
    pl.semaphore_wait(barrier, len(peers))

    def gather_y(k):
        return copy(blocks.at[row], blocks.at[row], ay_s.at[k], ay_r.at[k], at(dy=k))

    def landed_y(k):
        slot = blocks.at[x * ny + lax.rem(y + ny - k, ny)]
        return copy(slot, slot, ay_s.at[k], ay_r.at[k], at(dy=k))

    beside = sorted({1, nx - 1})

    def slot_of(dx, k):
        return blocks.at[lax.rem(x + nx - dx, nx) * ny + lax.rem(y + ny - k, ny)]

    def gather_x(k, m):
        slot = slot_of(0, k)
        return copy(slot, slot, ax_s.at[k, m], ax_r.at[k, m], at(dx=m))

    def landed_x(k, m):
        slot = slot_of(m, k)
        return copy(slot, slot, ax_s.at[k, m], ax_r.at[k, m], at(dx=m))

    def passed(k):
        return nx == 4 and min(k, ny - k) <= 2

    def relays(k, m):
        return passed(k) and m == (1 if k % 2 == 0 else 3)

    def pass_x(k):
        m = 1 if k % 2 == 0 else 3
        slot = slot_of(m, k)
        return copy(slot, slot, ax_s.at[k, 2], ax_r.at[k, 2], at(dx=m))

    def relay_x(k):
        if passed(k):
            landed_x(k, 1 if k % 2 == 0 else 3).wait_recv()
            pass_x(k).start()

    for k in near_first(ny):
        gather_y(k).start()
    for m in beside:
        gather_x(0, m).start()

    used = counts[0]
    lines = [coords[0, k] for k in range(slots)]

    def latest(line, below):
        found = jnp.int32(slots)
        for k in range(slots):
            found = jnp.where((lines[k] == line) & (k < below), k, found)
        return found

    def link(k, carry):
        table[k] = coords[1, k]
        table[slots + k] = latest(coords[0, k], k)
        return carry

    lax.fori_loop(0, slots, link, 0)

    def ends(r, carry):
        table[2 * slots + r] = latest(r, used)
        return carry

    lax.fori_loop(0, 2 * nz, ends, 0)

    for k in near_first(ny):
        landed_y(k).wait_recv()
        for m in beside if passed(k) or nx != 4 else [2] + beside:
            gather_x(k, m).start()
        if k == 1:
            relay_x(0)
    for k in near_first(ny):
        relay_x(k)
    for k in [0] + near_first(ny):
        for m in range(1, nx):
            if m not in beside or not relays(k, m):
                landed_x(k, m).wait_recv()
    get_tiles.wait()

    def product(g, carry):
        for u in range(4):
            k = g * 4 + u
            acc[k] = lax.dot_general(
                blocks[table[k]], tiles[k], NT, preferred_element_type=jnp.float32
            )
        return carry

    lax.fori_loop(0, slots // 4, product, 0)

    def chain(k, carry):
        acc[k] = acc[k] + acc[table[slots + k]]
        return carry

    lax.fori_loop(0, slots, chain, 0)

    def partial(d, core):
        return acc[table[2 * slots + lax.rem(z + d, nz) * 2 + core]]

    stages = []
    for n in range(half):
        stages += [d for d in (half - n, near - n) if (d > near and d == half - n) or (0 < d <= near and d == near - n)]
    order = []
    for d in stages:
        order += [d] if d == half else [d, 2 * half - d]
    order += [0]

    def swap(d):
        return copy(give.at[d], take.at[d], ex_s.at[d], ex_r.at[d], at(dc=1))

    for d in order:
        give[d] = partial(d, 1 - c)
        swap(d).start()

    def own(d):
        swap(d).wait_recv()
        return partial(d, c) + take[d]

    size = vecs // CHUNKS

    def hop(way, d, h):
        rows = pl.ds(h * size, size)
        dz = near + 1 if d == near + 1 else 1
        return copy(
            ring_out.at[way, d - 1, rows], ring_in.at[way, d - 1, rows], ring_s.at[way, d - 1, h],
            ring_r.at[way, d - 1, h], at(dz=dz if way == 0 else nz - dz),
        )

    def fresh(way, d):
        if d == half:
            return [h for h in range(CHUNKS) if (h < CHUNKS // 2) == (way == 0)]
        if d == half - 1:
            return [h for h in range(CHUNKS) if (h < CHUNKS // 2) != (way == 0)]
        return list(range(CHUNKS)) if d == near else []

    def carried(way, d):
        return [] if d == half else [h for h in range(CHUNKS) if h not in fresh(way, d)]

    for d in stages:
        if d == half:
            v = own(d)
            ring_out[0, d - 1, :part] = v[:part]
            ring_out[1, d - 1, part:] = v[part:]
        else:
            ring_out[0, d - 1] = own(d)
            ring_out[1, d - 1] = own(2 * half - d)
        for way in range(2):
            for h in fresh(way, d):
                hop(way, d, h).start()
    y_ref[...] = own(0)
    for d in stages:
        for h in range(CHUNKS):
            for way in range(2):
                if h in carried(way, d):
                    rows = pl.ds(h * size, size)
                    hop(way, d + 1, h).wait_recv()
                    ring_out[way, d - 1, rows] += ring_in[way, d, rows]
                    hop(way, d, h).start()
    for d in sorted({near + 1, 1}):
        for way in range(2):
            for h in range(CHUNKS):
                hop(way, d, h).wait_recv()
    whole = y_ref[...] + ring_in[0, 0] + ring_in[1, 0]
    if near > 0:
        whole = whole + ring_in[0, near] + ring_in[1, near]
    y_ref[...] = whole

    gram = lax.dot_general(whole, whole, NT, precision=HIGH, preferred_element_type=jnp.float32) * (1.0 / total)
    wide = jnp.concatenate([gram[:part], gram[part:]], axis=1)
    parts = nx * 2
    rows = part // parts
    mine = x * 2 + c
    for q in range(parts):
        pack[q] = wide[q * rows : (q + 1) * rows]

    around = [(dx, dc) for dx in range(nx) for dc in range(2) if (dx, dc) != (0, 0)]

    def place(dx, dc):
        return lax.rem(x + dx, nx) * 2 + lax.rem(c + dc, 2)

    def spread(dx, dc):
        n = dx * 2 + dc
        return copy(pack.at[place(dx, dc)], gin.at[mine], g_s.at[n], g_r.at[n], at(dx=dx, dc=dc))

    for dx, dc in around:
        spread(dx, dc).start()
    gin[mine] = pack[mine]
    for dx, dc in around:
        spread(dx, dc).wait_recv()
    s = gin[0]
    for q in range(1, parts):
        s = s + gin[q]
    yin[y] = s

    def over_y(k):
        return copy(yin.at[y], yin.at[y], gy_s.at[k], gy_r.at[k], at(dy=k))

    for k in far_first(ny):
        over_y(k).start()
    for k in range(1, ny):
        slot = yin.at[lax.rem(y + ny - k, ny)]
        copy(slot, slot, gy_s.at[k], gy_r.at[k], at(dy=k)).wait_recv()
    s = yin[0]
    for q in range(1, ny):
        s = s + yin[q]
    zin[z] = s

    def over_z(k):
        return copy(zin.at[z], zin.at[z], gz_s.at[k], gz_r.at[k], at(dz=k))

    for k in far_first(nz):
        over_z(k).start()
    for k in range(1, nz):
        slot = zin.at[lax.rem(z + nz - k, nz)]
        copy(slot, slot, gz_s.at[k], gz_r.at[k], at(dz=k)).wait_recv()
    s = zin[0]
    for q in range(1, nz):
        s = s + zin[q]
    gall[mine] = s

    def collect(dx, dc):
        n = dx * 2 + dc
        return copy(gall.at[mine], gall.at[mine], f_s.at[n], f_r.at[n], at(dx=dx, dc=dc))

    for dx, dc in around:
        collect(dx, dc).start()
    for dx, dc in around:
        n = dx * 2 + dc
        slot = gall.at[lax.rem(x + nx - dx, nx) * 2 + lax.rem(c + dc, 2)]
        copy(slot, slot, f_s.at[n], f_r.at[n], at(dx=dx, dc=dc)).wait_recv()
    for q in range(parts):
        gram_ref[q * rows : (q + 1) * rows] = gall[q]

    for k in range(1, ny):
        gather_y(k).wait_send()
        over_y(k).wait_send()
    for k in range(ny):
        for m in beside:
            gather_x(k, m).wait_send()
        if nx == 4:
            pass_x(k).wait_send()
    for k in range(1, nz):
        over_z(k).wait_send()
    for dx, dc in around:
        spread(dx, dc).wait_send()
        collect(dx, dc).wait_send()

    for d in order:
        swap(d).wait_send()
    for d in stages:
        for way in range(2):
            for h in fresh(way, d) + carried(way, d):
                hop(way, d, h).wait_send()


def orthonormal(gram_ref, y_hbm, basis_ref, factor_ref, y_ref, y_sem):
    n = y_ref.shape[0]
    get_y = pltpu.make_async_copy(y_hbm, y_ref, y_sem)
    get_y.start()
    half = n // 2
    packed = gram_ref[...]
    gram = jnp.concatenate([packed[:, :n], packed[:, n:]], axis=0)
    lane = lax.broadcasted_iota(jnp.int32, (n, n), 1)
    line = lax.broadcasted_iota(jnp.int32, (n, n), 0)
    work = jnp.concatenate([gram, (lane == line).astype(jnp.float32)], axis=1)
    groups = [work[g * 8 : (g + 1) * 8] for g in range(n // 8)]
    sub = lax.broadcasted_iota(jnp.int32, (8, 1), 0)
    for k in range(n):
        g, r = k // 8, k % 8
        pivot_row = groups[g][r : r + 1]
        scaled = pivot_row / pivot_row[:, k : k + 1]
        for i in range(g, n // 8):
            column = groups[i][:, k : k + 1]
            if i == g:
                column = jnp.where(sub > r, column, 0.0)
            groups[i] = groups[i] - column * scaled
    done = jnp.concatenate(groups, axis=0)
    diag = jnp.sum(jnp.where(lane == line, done[:, :n], 0.0), axis=1, keepdims=True)
    done = done / jnp.sqrt(diag)
    factor_ref[...] = jnp.where(lane >= line, done[:, :n], 0.0)
    get_y.wait()
    basis_ref[...] = jnp.dot(done[:, n:], y_ref[...], precision=HIGH, preferred_element_type=jnp.float32)


def local(dims, x_block, tiles, coords, counts):
    nx, ny, nz = dims
    vecs, width = x_block.shape
    slots = tiles.shape[0]
    half = nz // 2
    parts = nx * 2
    rows = vecs // 2 // parts
    total = width * nx * ny * nz * 2
    dma = pltpu.SemaphoreType.DMA
    f32 = jnp.float32
    gram, y = pl.pallas_call(
        functools.partial(exchange, dims, slots, total),
        name="exchange",
        out_shape=(jax.ShapeDtypeStruct((vecs // 2, 2 * vecs), f32), jax.ShapeDtypeStruct((vecs, width), f32)),
        in_specs=[
            pl.BlockSpec(memory_space=pltpu.SMEM),
            pl.BlockSpec(memory_space=pltpu.SMEM),
            pl.BlockSpec(memory_space=pltpu.HBM),
            pl.BlockSpec(memory_space=pltpu.HBM),
        ],
        out_specs=(pl.BlockSpec(memory_space=pltpu.VMEM), pl.BlockSpec(memory_space=pltpu.VMEM)),
        scratch_shapes=[
            pltpu.SMEM((2 * slots + 2 * nz,), jnp.int32),
            pltpu.VMEM((nx * ny, vecs, width), jnp.bfloat16),
            pltpu.VMEM(tiles.shape, jnp.bfloat16),
            pltpu.VMEM((slots + 1, vecs, width), f32),
            pltpu.VMEM((nz, vecs, width), f32),
            pltpu.VMEM((nz, vecs, width), f32),
            pltpu.VMEM((2, half, vecs, width), f32),
            pltpu.VMEM((2, half, vecs, width), f32),
            pltpu.VMEM((parts, rows, 2 * vecs), f32),
            pltpu.VMEM((parts, rows, 2 * vecs), f32),
            pltpu.VMEM((ny, rows, 2 * vecs), f32),
            pltpu.VMEM((nz, rows, 2 * vecs), f32),
            pltpu.VMEM((parts, rows, 2 * vecs), f32),
            dma((2,)),
            dma((ny,)), dma((ny,)),
            dma((ny, nx)), dma((ny, nx)),
            dma((nz,)), dma((nz,)),
            dma((2, half, CHUNKS)), dma((2, half, CHUNKS)),
            dma((parts,)), dma((parts,)),
            dma((ny,)), dma((ny,)),
            dma((nz,)), dma((nz,)),
            dma((parts,)), dma((parts,)),
        ],
        compiler_params=pltpu.CompilerParams(
            collective_id=0, has_side_effects=True, vmem_limit_bytes=62 * 1024 * 1024
        ),
    )(coords.T, counts, x_block, tiles)
    return pl.pallas_call(
        orthonormal,
        name="orthonormal",
        out_shape=(jax.ShapeDtypeStruct((vecs, width), f32), jax.ShapeDtypeStruct((vecs, vecs), f32)),
        in_specs=[pl.BlockSpec(memory_space=pltpu.VMEM), pl.BlockSpec(memory_space=pltpu.HBM)],
        out_specs=(pl.BlockSpec(memory_space=pltpu.VMEM), pl.BlockSpec(memory_space=pltpu.VMEM)),
        scratch_shapes=[pltpu.VMEM((vecs, width), f32), dma(())],
        compiler_params=pltpu.CompilerParams(vmem_limit_bytes=62 * 1024 * 1024),
    )(gram, y)


def solution(mesh):
    placed = (
        P(None, ("col", "row")),
        P(("row", "col"), None, None),
        P(("row", "col"), None),
        P(("row", "col")),
    )
    return jax.shard_map(
        functools.partial(local, DIMS),
        mesh=mesh,
        in_specs=placed,
        out_specs=(P(None, ("row", "col")), P()),
        check_vma=False,
    )
```

```python
import functools

import jax
import jax.numpy as jnp
from jax import lax
from jax.experimental import pallas as pl
from jax.experimental.pallas import tpu as pltpu
from jax.sharding import PartitionSpec as P

MESH = pl.DeviceIdType.MESH
HIGH = lax.Precision.HIGHEST
NT = (((1,), (1,)), ((), ()))
DIMS = (4, 8, 16)


NEAR = 3
CHUNKS = 4


def near_first(n):
    return sorted(range(1, n), key=lambda k: min(k, n - k))


def far_first(n):
    return near_first(n)[::-1]


def exchange(
    dims, slots, total, coords, counts, x_hbm, tiles_hbm, gram_ref, y_ref,
    table, blocks, tiles, acc, give, take, ring_out, ring_in, pack, gin, yin, zin, gall,
    local_sem, ay_s, ay_r, ax_s, ax_r, ex_s, ex_r, ring_s, ring_r, g_s, g_r, gy_s, gy_r, gz_s, gz_r, f_s, f_r,
):
    nx, ny, nz = dims
    half = nz // 2
    row, col = lax.axis_index("row"), lax.axis_index("col")
    x, y = row // ny, row % ny
    z, c = col // 2, col % 2
    vecs = y_ref.shape[0]
    part = vecs // 2

    def at(dx=0, dy=0, dz=0, dc=0):
        return (lax.rem(x + dx, nx) * ny + lax.rem(y + dy, ny), lax.rem(z + dz, nz) * 2 + lax.rem(c + dc, 2))

    def copy(src, dst, send, recv, dev):
        return pltpu.make_async_remote_copy(
            src_ref=src, dst_ref=dst, send_sem=send, recv_sem=recv, device_id=dev, device_id_type=MESH
        )

    near = max(0, min(NEAR, half - 2))
    peers = [at(dy=k) for k in range(1, ny)] + [at(dx=k) for k in range(1, nx)] + [at(dc=1)]
    peers += [at(dz=k) for k in sorted({1, near + 1, nz - near - 1, nz - 1})]
    barrier = pltpu.get_barrier_semaphore()
    for dev in peers:
        pl.semaphore_signal(barrier, inc=1, device_id=dev, device_id_type=MESH)
    get_x = pltpu.make_async_copy(x_hbm, blocks.at[row], local_sem.at[0])
    get_x.start()
    get_tiles = pltpu.make_async_copy(tiles_hbm, tiles, local_sem.at[1])
    get_tiles.start()
    acc[slots] = jnp.zeros_like(acc[slots])
    get_x.wait()
    pl.semaphore_wait(barrier, len(peers))

    def gather_y(k):
        return copy(blocks.at[row], blocks.at[row], ay_s.at[k], ay_r.at[k], at(dy=k))

    def landed_y(k):
        slot = blocks.at[x * ny + lax.rem(y + ny - k, ny)]
        return copy(slot, slot, ay_s.at[k], ay_r.at[k], at(dy=k))

    beside = sorted({1, nx - 1})
    corner = sorted({1, ny - 1})

    def slot_of(dx, k):
        return blocks.at[lax.rem(x + nx - dx, nx) * ny + lax.rem(y + ny - k, ny)]

    def gather_x(k, m):
        slot = slot_of(0, k)
        return copy(slot, slot, ax_s.at[k, m], ax_r.at[k, m], at(dx=m))

    def landed_x(k, m):
        slot = slot_of(m, k)
        return copy(slot, slot, ax_s.at[k, m], ax_r.at[k, m], at(dx=m))

    def turn(k, m):
        slot = slot_of(m, 0)
        return copy(slot, slot, ax_s.at[k, m], ax_r.at[k, m], at(dy=k))

    def passed(k):
        return nx == 4 and k not in corner and 0 < min(k, ny - k) <= 2

    def way_of(k):
        return 1 if 2 * k <= ny else nx - 1

    def relays(k, m):
        return passed(k) and m == way_of(k)

    def pass_x(k):
        m = way_of(k)
        slot = slot_of(m, k)
        return copy(slot, slot, ax_s.at[k, 2], ax_r.at[k, 2], at(dx=m))

    def relay_x(k):
        if passed(k):
            landed_x(k, way_of(k)).wait_recv()
            pass_x(k).start()

    for k in near_first(ny):
        gather_y(k).start()
    for m in range(1, nx):
        gather_x(0, m).start()

    used = counts[0]
    lines = [coords[0, k] for k in range(slots)]

    def latest(line, below):
        found = jnp.int32(slots)
        for k in range(slots):
            found = jnp.where((lines[k] == line) & (k < below), k, found)
        return found

    def link(k, carry):
        table[k] = coords[1, k]
        table[slots + k] = latest(coords[0, k], k)
        return carry

    lax.fori_loop(0, slots, link, 0)

    def ends(r, carry):
        table[2 * slots + r] = latest(r, used)
        return carry

    lax.fori_loop(0, 2 * nz, ends, 0)

    def move_on(k):
        landed_y(k).wait_recv()
        for m in beside if passed(k) else range(1, nx):
            gather_x(k, m).start()

    beyond = [k for k in near_first(ny) if k not in corner]
    for k in beyond[:2]:
        move_on(k)
    for m in range(1, nx):
        landed_x(0, m).wait_recv()
        for k in corner:
            turn(k, m).start()
    for k in beyond[2:]:
        move_on(k)
    for k in beyond:
        relay_x(k)
    for k in corner:
        landed_y(k).wait_recv()
    for k in near_first(ny):
        for m in range(1, nx):
            if not relays(k, m):
                landed_x(k, m).wait_recv()
    get_tiles.wait()

    def product(g, carry):
        for u in range(4):
            k = g * 4 + u
            acc[k] = lax.dot_general(
                blocks[table[k]], tiles[k], NT, preferred_element_type=jnp.float32
            )
        return carry

    lax.fori_loop(0, slots // 4, product, 0)

    def chain(k, carry):
        acc[k] = acc[k] + acc[table[slots + k]]
        return carry

    lax.fori_loop(0, slots, chain, 0)

    def partial(d, core):
        return acc[table[2 * slots + lax.rem(z + d, nz) * 2 + core]]

    stages = []
    for n in range(half):
        stages += [d for d in (half - n, near - n) if (d > near and d == half - n) or (0 < d <= near and d == near - n)]
    order = []
    for d in stages:
        order += [d] if d == half else [d, 2 * half - d]
    order += [0]

    def swap(d):
        return copy(give.at[d], take.at[d], ex_s.at[d], ex_r.at[d], at(dc=1))

    for d in order:
        give[d] = partial(d, 1 - c)
        swap(d).start()

    def own(d):
        swap(d).wait_recv()
        return partial(d, c) + take[d]

    size = vecs // CHUNKS

    def hop(way, d, h):
        rows = pl.ds(h * size, size)
        dz = near + 1 if d == near + 1 else 1
        return copy(
            ring_out.at[way, d - 1, rows], ring_in.at[way, d - 1, rows], ring_s.at[way, d - 1, h],
            ring_r.at[way, d - 1, h], at(dz=dz if way == 0 else nz - dz),
        )

    def fresh(way, d):
        if d == half:
            return [h for h in range(CHUNKS) if (h < CHUNKS // 2) == (way == 0)]
        if d == half - 1:
            return [h for h in range(CHUNKS) if (h < CHUNKS // 2) != (way == 0)]
        return list(range(CHUNKS)) if d == near else []

    def carried(way, d):
        return [] if d == half else [h for h in range(CHUNKS) if h not in fresh(way, d)]

    for d in stages:
        if d == half:
            v = own(d)
            ring_out[0, d - 1, :part] = v[:part]
            ring_out[1, d - 1, part:] = v[part:]
        else:
            ring_out[0, d - 1] = own(d)
            ring_out[1, d - 1] = own(2 * half - d)
        for way in range(2):
            for h in fresh(way, d):
                hop(way, d, h).start()
    y_ref[...] = own(0)
    for d in stages:
        for h in range(CHUNKS):
            for way in range(2):
                if h in carried(way, d):
                    rows = pl.ds(h * size, size)
                    hop(way, d + 1, h).wait_recv()
                    ring_out[way, d - 1, rows] += ring_in[way, d, rows]
                    hop(way, d, h).start()
    for d in sorted({near + 1, 1}):
        for way in range(2):
            for h in range(CHUNKS):
                hop(way, d, h).wait_recv()
    whole = y_ref[...] + ring_in[0, 0] + ring_in[1, 0]
    if near > 0:
        whole = whole + ring_in[0, near] + ring_in[1, near]
    y_ref[...] = whole

    gram = lax.dot_general(whole, whole, NT, precision=HIGH, preferred_element_type=jnp.float32) * (1.0 / total)
    wide = jnp.concatenate([gram[:part], gram[part:]], axis=1)
    parts = nx * 2
    rows = part // parts
    mine = x * 2 + c
    for q in range(parts):
        pack[q] = wide[q * rows : (q + 1) * rows]

    around = [(dx, dc) for dx in range(nx) for dc in range(2) if (dx, dc) != (0, 0)]

    def place(dx, dc):
        return lax.rem(x + dx, nx) * 2 + lax.rem(c + dc, 2)

    def spread(dx, dc):
        n = dx * 2 + dc
        return copy(pack.at[place(dx, dc)], gin.at[mine], g_s.at[n], g_r.at[n], at(dx=dx, dc=dc))

    for dx, dc in around:
        spread(dx, dc).start()
    gin[mine] = pack[mine]
    for dx, dc in around:
        spread(dx, dc).wait_recv()
    s = gin[0]
    for q in range(1, parts):
        s = s + gin[q]
    yin[y] = s

    def over_y(k):
        return copy(yin.at[y], yin.at[y], gy_s.at[k], gy_r.at[k], at(dy=k))

    for k in far_first(ny):
        over_y(k).start()
    for k in range(1, ny):
        slot = yin.at[lax.rem(y + ny - k, ny)]
        copy(slot, slot, gy_s.at[k], gy_r.at[k], at(dy=k)).wait_recv()
    s = yin[0]
    for q in range(1, ny):
        s = s + yin[q]
    zin[z] = s

    def over_z(k):
        return copy(zin.at[z], zin.at[z], gz_s.at[k], gz_r.at[k], at(dz=k))

    for k in far_first(nz):
        over_z(k).start()
    for k in range(1, nz):
        slot = zin.at[lax.rem(z + nz - k, nz)]
        copy(slot, slot, gz_s.at[k], gz_r.at[k], at(dz=k)).wait_recv()
    s = zin[0]
    for q in range(1, nz):
        s = s + zin[q]
    gall[mine] = s

    def collect(dx, dc):
        n = dx * 2 + dc
        return copy(gall.at[mine], gall.at[mine], f_s.at[n], f_r.at[n], at(dx=dx, dc=dc))

    for dx, dc in around:
        collect(dx, dc).start()
    for dx, dc in around:
        n = dx * 2 + dc
        slot = gall.at[lax.rem(x + nx - dx, nx) * 2 + lax.rem(c + dc, 2)]
        copy(slot, slot, f_s.at[n], f_r.at[n], at(dx=dx, dc=dc)).wait_recv()
    for q in range(parts):
        gram_ref[q * rows : (q + 1) * rows] = gall[q]

    for k in range(1, ny):
        gather_y(k).wait_send()
        over_y(k).wait_send()
    for k in range(ny):
        for m in range(1, nx):
            if k in corner:
                turn(k, m).wait_send()
            elif m in beside or not passed(k):
                gather_x(k, m).wait_send()
        if passed(k):
            pass_x(k).wait_send()
    for k in range(1, nz):
        over_z(k).wait_send()
    for dx, dc in around:
        spread(dx, dc).wait_send()
        collect(dx, dc).wait_send()

    for d in order:
        swap(d).wait_send()
    for d in stages:
        for way in range(2):
            for h in fresh(way, d) + carried(way, d):
                hop(way, d, h).wait_send()


def orthonormal(gram_ref, y_hbm, basis_ref, factor_ref, y_ref, y_sem):
    n = y_ref.shape[0]
    get_y = pltpu.make_async_copy(y_hbm, y_ref, y_sem)
    get_y.start()
    packed = gram_ref[...]
    gram = jnp.concatenate([packed[:, :n], packed[:, n:]], axis=0)
    lane = lax.broadcasted_iota(jnp.int32, (n, n), 1)
    line = lax.broadcasted_iota(jnp.int32, (n, n), 0)
    work = jnp.concatenate([gram, (lane == line).astype(jnp.float32)], axis=1)
    groups = [work[g * 8 : (g + 1) * 8] for g in range(n // 8)]
    sub = lax.broadcasted_iota(jnp.int32, (8, 2 * n), 0)
    full = (8, 2 * n)
    for g in range(n // 8):
        first = g * 8
        block = groups[g]
        rows = [jnp.broadcast_to(block[r : r + 1], full) for r in range(8)]
        small = [
            [jnp.broadcast_to(rows[r][:, first + q : first + q + 1], full) if q >= r else None for q in range(8)]
            for r in range(8)
        ]
        times = [[None] * 8 for _ in range(8)]
        inverse = []
        for r in range(8):
            inverse.append(1.0 / small[r][r])
            for q in range(r + 1, 8):
                times[q][r] = small[r][q] * inverse[r]
            for i in range(r + 1, 8):
                for q in range(i, 8):
                    small[i][q] = small[i][q] - times[i][r] * small[r][q]
                rows[i] = rows[i] - times[i][r] * rows[r]
        block = rows[0]
        for r in range(1, 8):
            block = jnp.where(sub == r, rows[r], block)
        groups[g] = block
        scaled = [rows[r] * inverse[r] for r in range(8)]
        for i in range(g + 1, n // 8):
            block = groups[i]
            left = [jnp.broadcast_to(block[:, first + r : first + r + 1], full) for r in range(8)]
            for r in range(8):
                block = block - left[r] * scaled[r]
                for q in range(r + 1, 8):
                    left[q] = left[q] - left[r] * times[q][r]
            groups[i] = block
    done = jnp.concatenate(groups, axis=0)
    diag = jnp.sum(jnp.where(lane == line, done[:, :n], 0.0), axis=1, keepdims=True)
    done = done / jnp.sqrt(diag)
    factor_ref[...] = jnp.where(lane >= line, done[:, :n], 0.0)
    get_y.wait()
    basis_ref[...] = jnp.dot(done[:, n:], y_ref[...], precision=HIGH, preferred_element_type=jnp.float32)


def local(dims, x_block, tiles, coords, counts):
    nx, ny, nz = dims
    vecs, width = x_block.shape
    slots = tiles.shape[0]
    half = nz // 2
    parts = nx * 2
    rows = vecs // 2 // parts
    total = width * nx * ny * nz * 2
    dma = pltpu.SemaphoreType.DMA
    f32 = jnp.float32
    gram, y = pl.pallas_call(
        functools.partial(exchange, dims, slots, total),
        name="exchange",
        out_shape=(jax.ShapeDtypeStruct((vecs // 2, 2 * vecs), f32), jax.ShapeDtypeStruct((vecs, width), f32)),
        in_specs=[
            pl.BlockSpec(memory_space=pltpu.SMEM),
            pl.BlockSpec(memory_space=pltpu.SMEM),
            pl.BlockSpec(memory_space=pltpu.HBM),
            pl.BlockSpec(memory_space=pltpu.HBM),
        ],
        out_specs=(pl.BlockSpec(memory_space=pltpu.VMEM), pl.BlockSpec(memory_space=pltpu.VMEM)),
        scratch_shapes=[
            pltpu.SMEM((2 * slots + 2 * nz,), jnp.int32),
            pltpu.VMEM((nx * ny, vecs, width), jnp.bfloat16),
            pltpu.VMEM(tiles.shape, jnp.bfloat16),
            pltpu.VMEM((slots + 1, vecs, width), f32),
            pltpu.VMEM((nz, vecs, width), f32),
            pltpu.VMEM((nz, vecs, width), f32),
            pltpu.VMEM((2, half, vecs, width), f32),
            pltpu.VMEM((2, half, vecs, width), f32),
            pltpu.VMEM((parts, rows, 2 * vecs), f32),
            pltpu.VMEM((parts, rows, 2 * vecs), f32),
            pltpu.VMEM((ny, rows, 2 * vecs), f32),
            pltpu.VMEM((nz, rows, 2 * vecs), f32),
            pltpu.VMEM((parts, rows, 2 * vecs), f32),
            dma((2,)),
            dma((ny,)), dma((ny,)),
            dma((ny, nx)), dma((ny, nx)),
            dma((nz,)), dma((nz,)),
            dma((2, half, CHUNKS)), dma((2, half, CHUNKS)),
            dma((parts,)), dma((parts,)),
            dma((ny,)), dma((ny,)),
            dma((nz,)), dma((nz,)),
            dma((parts,)), dma((parts,)),
        ],
        compiler_params=pltpu.CompilerParams(
            collective_id=0, has_side_effects=True, vmem_limit_bytes=62 * 1024 * 1024
        ),
    )(coords.T, counts, x_block, tiles)
    return pl.pallas_call(
        orthonormal,
        name="orthonormal",
        out_shape=(jax.ShapeDtypeStruct((vecs, width), f32), jax.ShapeDtypeStruct((vecs, vecs), f32)),
        in_specs=[pl.BlockSpec(memory_space=pltpu.VMEM), pl.BlockSpec(memory_space=pltpu.HBM)],
        out_specs=(pl.BlockSpec(memory_space=pltpu.VMEM), pl.BlockSpec(memory_space=pltpu.VMEM)),
        scratch_shapes=[pltpu.VMEM((vecs, width), f32), dma(())],
        compiler_params=pltpu.CompilerParams(vmem_limit_bytes=62 * 1024 * 1024),
    )(gram, y)


def solution(mesh):
    placed = (
        P(None, ("col", "row")),
        P(("row", "col"), None, None),
        P(("row", "col"), None),
        P(("row", "col")),
    )
    return jax.shard_map(
        functools.partial(local, DIMS),
        mesh=mesh,
        in_specs=placed,
        out_specs=(P(None, ("row", "col")), P()),
        check_vma=False,
    )
```

```python
import functools

import jax
import jax.numpy as jnp
from jax import lax
from jax.experimental import pallas as pl
from jax.experimental.pallas import tpu as pltpu
from jax.sharding import PartitionSpec as P

MESH = pl.DeviceIdType.MESH
HIGH = lax.Precision.HIGHEST
NT = (((1,), (1,)), ((), ()))
DIMS = (4, 8, 16)


NEAR = 3
CHUNKS = (2, 1)


def near_first(n):
    return sorted(range(1, n), key=lambda k: min(k, n - k))


def far_first(n):
    return near_first(n)[::-1]


def exchange(
    dims, slots, total, coords, counts, x_hbm, tiles_hbm, gram_ref, y_hbm,
    table, y_ref, blocks, tiles, acc, give, take, ring_out, ring_in, pack, gin, yin, zin, gall,
    local_sem, ay_s, ay_r, ax_s, ax_r, ex_s, ex_r, ring_s, ring_r, g_s, g_r, gy_s, gy_r, gz_s, gz_r, f_s, f_r,
):
    nx, ny, nz = dims
    half = nz // 2
    row, col = lax.axis_index("row"), lax.axis_index("col")
    x, y = row // ny, row % ny
    z, c = col // 2, col % 2
    vecs = y_ref.shape[0]
    part = vecs // 2

    known = {}

    def at(dx=0, dy=0, dz=0, dc=0):
        if (dx, dy, dz, dc) not in known:
            known[dx, dy, dz, dc] = place_of(dx, dy, dz, dc)
        return known[dx, dy, dz, dc]

    def place_of(dx, dy, dz, dc):
        return (lax.rem(x + dx, nx) * ny + lax.rem(y + dy, ny), lax.rem(z + dz, nz) * 2 + lax.rem(c + dc, 2))

    def copy(src, dst, send, recv, dev):
        return pltpu.make_async_remote_copy(
            src_ref=src, dst_ref=dst, send_sem=send, recv_sem=recv, device_id=dev, device_id_type=MESH
        )

    near = max(0, min(NEAR, half - 2))
    peers = [at(dy=k) for k in range(1, ny)] + [at(dx=k) for k in range(1, nx)] + [at(dc=1)]
    peers += [at(dz=k) for k in sorted({1, near + 1, nz - near - 1, nz - 1})]
    barrier = pltpu.get_barrier_semaphore()
    for dev in peers:
        pl.semaphore_signal(barrier, inc=1, device_id=dev, device_id_type=MESH)
    get_x = pltpu.make_async_copy(x_hbm, blocks.at[row], local_sem.at[0])
    get_x.start()
    get_tiles = pltpu.make_async_copy(tiles_hbm, tiles, local_sem.at[1])
    get_tiles.start()
    acc[slots] = jnp.zeros_like(acc[slots])
    get_x.wait()
    pl.semaphore_wait(barrier, len(peers))

    def gather_y(k):
        return copy(blocks.at[row], blocks.at[row], ay_s.at[k], ay_r.at[k], at(dy=k))

    def landed_y(k):
        slot = blocks.at[x * ny + lax.rem(y + ny - k, ny)]
        return copy(slot, slot, ay_s.at[k], ay_r.at[k], at(dy=k))

    beside = sorted({1, nx - 1})
    corner = sorted({1, ny - 1})

    def slot_of(dx, k):
        return blocks.at[lax.rem(x + nx - dx, nx) * ny + lax.rem(y + ny - k, ny)]

    def gather_x(k, m):
        slot = slot_of(0, k)
        return copy(slot, slot, ax_s.at[k, m], ax_r.at[k, m], at(dx=m))

    def landed_x(k, m):
        slot = slot_of(m, k)
        return copy(slot, slot, ax_s.at[k, m], ax_r.at[k, m], at(dx=m))

    def turn(k, m):
        slot = slot_of(m, 0)
        return copy(slot, slot, ax_s.at[k, m], ax_r.at[k, m], at(dy=k))

    def passed(k):
        return nx == 4 and k not in corner and 0 < min(k, ny - k) <= 2

    def way_of(k):
        return 1 if 2 * k <= ny else nx - 1

    def relays(k, m):
        return passed(k) and m == way_of(k)

    def pass_x(k):
        m = way_of(k)
        slot = slot_of(m, k)
        return copy(slot, slot, ax_s.at[k, 2], ax_r.at[k, 2], at(dx=m))

    def relay_x(k):
        if passed(k):
            landed_x(k, way_of(k)).wait_recv()
            pass_x(k).start()

    beyond = [k for k in near_first(ny) if k not in corner]
    for m in far_first(nx):
        gather_x(0, m).start()
    for k in beyond + corner:
        gather_y(k).start()

    used = counts[0]
    lines = [coords[0, k] for k in range(slots)]

    def latest(line, below):
        found = jnp.int32(slots)
        for k in range(slots):
            found = jnp.where((lines[k] == line) & (k < below), k, found)
        return found

    def link(k, carry):
        table[k] = coords[1, k]
        table[slots + k] = latest(coords[0, k], k)
        return carry

    lax.fori_loop(0, slots, link, 0)

    def move_on(k):
        landed_y(k).wait_recv()
        for m in beside if passed(k) else range(1, nx):
            gather_x(k, m).start()

    for k in beyond[:2]:
        move_on(k)
    for m in range(1, nx):
        landed_x(0, m).wait_recv()
        for k in corner:
            turn(k, m).start()
    for k in beyond[2:]:
        move_on(k)

    def ends(r, carry):
        table[2 * slots + r] = latest(r, used)
        return carry

    lax.fori_loop(0, 2 * nz, ends, 0)

    for k in beyond:
        relay_x(k)
    for k in corner:
        landed_y(k).wait_recv()
    for k in near_first(ny):
        for m in range(1, nx):
            if not relays(k, m):
                landed_x(k, m).wait_recv()
    get_tiles.wait()

    def product(g, carry):
        for u in range(4):
            k = g * 4 + u
            acc[k] = lax.dot_general(
                blocks[table[k]], tiles[k], NT, preferred_element_type=jnp.float32
            )
        return carry

    lax.fori_loop(0, slots // 4, product, 0)

    def chain(g, carry):
        for u in range(4):
            k = g * 4 + u
            acc[k] = acc[k] + acc[table[slots + k]]
        return carry

    lax.fori_loop(0, slots // 4, chain, 0)

    def partial(d, core):
        return acc[table[2 * slots + lax.rem(z + d, nz) * 2 + core]]

    far = list(range(half, near, -1))
    stages = far[:2]
    for n in range(max(len(far) - 2, near)):
        stages += [near - n] * (n < near) + far[n + 2 : n + 3]
    order = []
    for d in stages:
        order += [d] if d == half else [d, 2 * half - d]
    order += [0]

    def swap(d):
        return copy(give.at[d], take.at[d], ex_s.at[d], ex_r.at[d], at(dc=1))

    for d in order:
        give[d] = partial(d, 1 - c)
        swap(d).start()

    def own(d):
        swap(d).wait_recv()
        return partial(d, c) + take[d]

    def count(d):
        return CHUNKS[0 if d > near else 1]

    def lines_of(d, h):
        size = vecs // count(d)
        return pl.ds(h * size, size)

    def hop(way, d, h):
        dz = near + 1 if d == near + 1 else 1
        return copy(
            ring_out.at[way, d - 1, lines_of(d, h)], ring_in.at[way, d - 1, lines_of(d, h)], ring_s.at[way, d - 1, h],
            ring_r.at[way, d - 1, h], at(dz=dz if way == 0 else nz - dz),
        )

    def fresh(way, d):
        every = range(count(d))
        if d == half:
            return [h for h in every if (h < count(d) // 2) == (way == 0)]
        if d == half - 1:
            return [h for h in every if (h < count(d) // 2) != (way == 0)]
        return list(every) if d == near else []

    def carried(way, d):
        return [] if d == half else [h for h in range(count(d)) if h not in fresh(way, d)]

    for d in stages:
        if d == half:
            v = own(d)
            ring_out[0, d - 1, :part] = v[:part]
            ring_out[1, d - 1, part:] = v[part:]
        else:
            ring_out[0, d - 1] = own(d)
            ring_out[1, d - 1] = own(2 * half - d)
        for way in range(2):
            for h in fresh(way, d):
                hop(way, d, h).start()
    y_ref[...] = own(0)
    for d in stages:
        for h in range(count(d)):
            for way in range(2):
                if h in carried(way, d):
                    rows = lines_of(d, h)
                    hop(way, d + 1, h).wait_recv()
                    ring_out[way, d - 1, rows] += ring_in[way, d, rows]
                    hop(way, d, h).start()
    for d in sorted({near + 1, 1}):
        for way in range(2):
            for h in range(count(d)):
                hop(way, d, h).wait_recv()
    whole = y_ref[...] + ring_in[0, 0] + ring_in[1, 0]
    if near > 0:
        whole = whole + ring_in[0, near] + ring_in[1, near]
    y_ref[...] = whole
    put_y = pltpu.make_async_copy(y_ref, y_hbm, local_sem.at[0])
    put_y.start()

    gram = lax.dot_general(whole, whole, NT, precision=HIGH, preferred_element_type=jnp.float32) * (1.0 / total)
    wide = jnp.concatenate([gram[:part], gram[part:]], axis=1)
    parts = nx * 2
    rows = part // parts
    mine = x * 2 + c
    for q in range(parts):
        pack[q] = wide[q * rows : (q + 1) * rows]

    around = [(dx, dc) for dx in range(nx) for dc in range(2) if (dx, dc) != (0, 0)]

    def place(dx, dc):
        return lax.rem(x + dx, nx) * 2 + lax.rem(c + dc, 2)

    def spread(dx, dc):
        n = dx * 2 + dc
        return copy(pack.at[place(dx, dc)], gin.at[mine], g_s.at[n], g_r.at[n], at(dx=dx, dc=dc))

    for dx, dc in around:
        spread(dx, dc).start()
    gin[mine] = pack[mine]
    for dx, dc in around:
        spread(dx, dc).wait_recv()
    s = gin[0]
    for q in range(1, parts):
        s = s + gin[q]
    yin[y] = s

    def over_y(k):
        return copy(yin.at[y], yin.at[y], gy_s.at[k], gy_r.at[k], at(dy=k))

    for k in far_first(ny):
        over_y(k).start()
    for k in range(1, ny):
        slot = yin.at[lax.rem(y + ny - k, ny)]
        copy(slot, slot, gy_s.at[k], gy_r.at[k], at(dy=k)).wait_recv()
    s = yin[0]
    for q in range(1, ny):
        s = s + yin[q]
    zin[z] = s

    def over_z(k):
        return copy(zin.at[z], zin.at[z], gz_s.at[k], gz_r.at[k], at(dz=k))

    for k in far_first(nz):
        over_z(k).start()
    for k in range(1, ny):
        gather_y(k).wait_send()
        over_y(k).wait_send()
    for k in range(ny):
        for m in range(1, nx):
            if k in corner:
                turn(k, m).wait_send()
            elif m in beside or not passed(k):
                gather_x(k, m).wait_send()
        if passed(k):
            pass_x(k).wait_send()
    for dx, dc in around:
        spread(dx, dc).wait_send()
    for d in order:
        swap(d).wait_send()
    for d in stages:
        for way in range(2):
            for h in fresh(way, d) + carried(way, d):
                hop(way, d, h).wait_send()
    for k in range(1, nz):
        slot = zin.at[lax.rem(z + nz - k, nz)]
        copy(slot, slot, gz_s.at[k], gz_r.at[k], at(dz=k)).wait_recv()
    s = zin[0]
    for q in range(1, nz):
        s = s + zin[q]
    gall[mine] = s

    def collect(dx, dc):
        n = dx * 2 + dc
        return copy(gall.at[mine], gall.at[mine], f_s.at[n], f_r.at[n], at(dx=dx, dc=dc))

    for dx, dc in around:
        collect(dx, dc).start()
    for dx, dc in around:
        n = dx * 2 + dc
        slot = gall.at[lax.rem(x + nx - dx, nx) * 2 + lax.rem(c + dc, 2)]
        copy(slot, slot, f_s.at[n], f_r.at[n], at(dx=dx, dc=dc)).wait_recv()
    for q in range(parts):
        gram_ref[q * rows : (q + 1) * rows] = gall[q]

    for k in range(1, nz):
        over_z(k).wait_send()
    for dx, dc in around:
        collect(dx, dc).wait_send()
    put_y.wait()


def orthonormal(gram_ref, y_hbm, basis_ref, factor_ref, y_ref, y_sem):
    n = y_ref.shape[0]
    get_y = pltpu.make_async_copy(y_hbm, y_ref, y_sem)
    get_y.start()
    packed = gram_ref[...]
    gram = jnp.concatenate([packed[:, :n], packed[:, n:]], axis=0)
    lane = lax.broadcasted_iota(jnp.int32, (n, n), 1)
    line = lax.broadcasted_iota(jnp.int32, (n, n), 0)
    work = jnp.concatenate([gram, (lane == line).astype(jnp.float32)], axis=1)
    groups = [work[g * 8 : (g + 1) * 8] for g in range(n // 8)]
    sub = lax.broadcasted_iota(jnp.int32, (8, 2 * n), 0)
    full = (8, 2 * n)
    for g in range(n // 8):
        first = g * 8
        block = groups[g]
        rows = [jnp.broadcast_to(block[r : r + 1], full) for r in range(8)]
        small = [
            [jnp.broadcast_to(rows[r][:, first + q : first + q + 1], full) if q >= r else None for q in range(8)]
            for r in range(8)
        ]
        times = [[None] * 8 for _ in range(8)]
        inverse = []
        for r in range(8):
            inverse.append(1.0 / small[r][r])
            for q in range(r + 1, 8):
                times[q][r] = small[r][q] * inverse[r]
            for i in range(r + 1, 8):
                for q in range(i, 8):
                    small[i][q] = small[i][q] - times[i][r] * small[r][q]
                rows[i] = rows[i] - times[i][r] * rows[r]
        block = rows[0]
        for r in range(1, 8):
            block = jnp.where(sub == r, rows[r], block)
        groups[g] = block
        scaled = [rows[r] * inverse[r] for r in range(8)]
        for i in range(g + 1, n // 8):
            block = groups[i]
            left = [jnp.broadcast_to(block[:, first + r : first + r + 1], full) for r in range(8)]
            for r in range(8):
                block = block - left[r] * scaled[r]
                for q in range(r + 1, 8):
                    left[q] = left[q] - left[r] * times[q][r]
            groups[i] = block
    done = jnp.concatenate(groups, axis=0)
    diag = jnp.sum(jnp.where(lane == line, done[:, :n], 0.0), axis=1, keepdims=True)
    done = done / jnp.sqrt(diag)
    factor_ref[...] = jnp.where(lane >= line, done[:, :n], 0.0)
    get_y.wait()
    basis_ref[...] = jnp.dot(done[:, n:], y_ref[...], precision=HIGH, preferred_element_type=jnp.float32)


def local(dims, x_block, tiles, coords, counts):
    nx, ny, nz = dims
    vecs, width = x_block.shape
    slots = tiles.shape[0]
    half = nz // 2
    parts = nx * 2
    rows = vecs // 2 // parts
    total = width * nx * ny * nz * 2
    dma = pltpu.SemaphoreType.DMA
    f32 = jnp.float32
    gram, y = pl.pallas_call(
        functools.partial(exchange, dims, slots, total),
        name="exchange",
        out_shape=(jax.ShapeDtypeStruct((vecs // 2, 2 * vecs), f32), jax.ShapeDtypeStruct((vecs, width), f32)),
        in_specs=[
            pl.BlockSpec(memory_space=pltpu.SMEM),
            pl.BlockSpec(memory_space=pltpu.SMEM),
            pl.BlockSpec(memory_space=pltpu.HBM),
            pl.BlockSpec(memory_space=pltpu.HBM),
        ],
        out_specs=(pl.BlockSpec(memory_space=pltpu.VMEM), pl.BlockSpec(memory_space=pltpu.HBM)),
        scratch_shapes=[
            pltpu.SMEM((2 * slots + 2 * nz,), jnp.int32),
            pltpu.VMEM((vecs, width), f32),
            pltpu.VMEM((nx * ny, vecs, width), jnp.bfloat16),
            pltpu.VMEM(tiles.shape, jnp.bfloat16),
            pltpu.VMEM((slots + 1, vecs, width), f32),
            pltpu.VMEM((nz, vecs, width), f32),
            pltpu.VMEM((nz, vecs, width), f32),
            pltpu.VMEM((2, half, vecs, width), f32),
            pltpu.VMEM((2, half, vecs, width), f32),
            pltpu.VMEM((parts, rows, 2 * vecs), f32),
            pltpu.VMEM((parts, rows, 2 * vecs), f32),
            pltpu.VMEM((ny, rows, 2 * vecs), f32),
            pltpu.VMEM((nz, rows, 2 * vecs), f32),
            pltpu.VMEM((parts, rows, 2 * vecs), f32),
            dma((2,)),
            dma((ny,)), dma((ny,)),
            dma((ny, nx)), dma((ny, nx)),
            dma((nz,)), dma((nz,)),
            dma((2, half, max(CHUNKS))), dma((2, half, max(CHUNKS))),
            dma((parts,)), dma((parts,)),
            dma((ny,)), dma((ny,)),
            dma((nz,)), dma((nz,)),
            dma((parts,)), dma((parts,)),
        ],
        compiler_params=pltpu.CompilerParams(
            collective_id=0, has_side_effects=True, vmem_limit_bytes=62 * 1024 * 1024
        ),
    )(coords.T, counts, x_block, tiles)
    return pl.pallas_call(
        orthonormal,
        name="orthonormal",
        out_shape=(jax.ShapeDtypeStruct((vecs, width), f32), jax.ShapeDtypeStruct((vecs, vecs), f32)),
        in_specs=[pl.BlockSpec(memory_space=pltpu.VMEM), pl.BlockSpec(memory_space=pltpu.HBM)],
        out_specs=(pl.BlockSpec(memory_space=pltpu.VMEM), pl.BlockSpec(memory_space=pltpu.VMEM)),
        scratch_shapes=[pltpu.VMEM((vecs, width), f32), dma(())],
        compiler_params=pltpu.CompilerParams(vmem_limit_bytes=62 * 1024 * 1024),
    )(gram, y)


def solution(mesh):
    placed = (
        P(None, ("col", "row")),
        P(("row", "col"), None, None),
        P(("row", "col"), None),
        P(("row", "col")),
    )
    return jax.shard_map(
        functools.partial(local, DIMS),
        mesh=mesh,
        in_specs=placed,
        out_specs=(P(None, ("row", "col")), P()),
        check_vma=False,
    )
```
